32 devices in a mesh: groups: 2 (over x), fibre: 16 (over z, y, core).
Axes of the slice: x: 2, y: 2, z: 4, core: 2. Of those that a mesh axis runs over, the one named last changes fastest.
Arguments:
- traces: bfloat16 [2048, 4096], P(('groups', 'fibre')), parts along dimension 0, may hold values from -6 to 6
- alive: int32 [2048], P(('groups', 'fibre')), parts along dimension 0, may hold values 0 or 1
- offsets: int32 [3], replicated, may hold values from 1 to 256, as said below
- probe: bfloat16 [4096, 64], replicated, may hold values from -0.09375 to 0.09375
Outputs:
- correlations: bfloat16 [3, 2048, 4096], P(None, ('groups', 'fibre')), parts along dimension 1
- denoised: bfloat16 [3, 2048, 4096], P(None, ('groups', 'fibre')), parts along dimension 1
The draws below stay inside these ranges and needn't reach their ends.
There are 2 independent parts, one for each index of `groups`. The reference program is written for one: setup_inputs(seed, part) draws one part's arguments, and reference() takes and returns one part's arrays. A program takes and returns all parts, laid end to end along the dimension named above; an argument that names none is the same for every part. Nothing has to cross between parts.
Inputs may be any that keep to these rules, and one draw needn't show every extreme that they name: 3 distinct offsets, one of them equal to 256.
All inputs are finite; a program needn't handle non-finite values. No bound on the sum of `alive` on one device may be relied on, other than what follows from the above.
Results may differ from the reference program's by a relative error of at most 0.028.
Values may be sent and summed in bfloat16 or wider, within the bound.
A program may use at most 64 MiB of HBM per device.

```python
import jax
import jax.numpy as jnp
from jax import lax

NT = 4096
RANK = 64
WINDOW = 256
NOFF = 3
CHANNELS = 1024


def draw_offsets(key, part):
    others = jax.random.permutation(key, WINDOW - 1)[:NOFF - 1] + 1
    return jnp.concatenate([others.astype(jnp.int32), jnp.full((1,), WINDOW, jnp.int32)])


def touch_ends(result, stream_key, least, high):
    longest = result.shape.index(max(result.shape))
    spots = []
    for shift in (0, 1):
        where = [jax.random.randint(jax.random.fold_in(stream_key, axis), (), 0, length) for axis, length in enumerate(result.shape)]
        where[longest] = (where[longest] + shift) % result.shape[longest]
        spots.append(tuple(where))
    return result.at[spots[0]].set(least).at[spots[1]].set(high)


def block_levels(own_key, extent, cuts, smallest, largest):
    factor_of = 1.0
    for axis_at, parts in cuts:
        heights = jax.random.uniform(jax.random.fold_in(jax.random.fold_in(own_key, 6), axis_at), (parts,), jnp.float32, smallest / len(cuts), largest / len(cuts))
        factor_of = factor_of * jnp.repeat(jnp.exp(heights), extent[axis_at] // parts).reshape((-1,) + (1,) * (len(extent) - 1 - axis_at))
    return factor_of


def centred(rng, extent, width, limit, split=(), kind=jnp.bfloat16):
    array = width * jax.random.normal(rng, extent, jnp.float32)
    if split:
        array = array * block_levels(rng, extent, split, -0.22, 0.18)
    return jnp.clip(array, -limit, limit).astype(kind)


def setup_inputs(seed: int = 0, part: int = 0) -> dict:
    splits = jax.random.split(jax.random.key(seed), 5)
    part_keys = jax.random.split(jax.random.fold_in(splits[4], part), 5)
    traces = centred(part_keys[0], (CHANNELS, NT), 1.0, 6.0, ((0, 16),))
    alive = touch_ends((jax.random.randint(part_keys[1], (CHANNELS,), 0, 8) < 7).astype(jnp.int32), jax.random.fold_in(part_keys[1], 1), 0, 1)
    offsets = draw_offsets(jax.random.fold_in(splits[4], 71), part)
    probe = centred(splits[3], (NT, RANK), NT ** -0.5, 0.09375)
    return {"traces": traces, "alive": alive, "offsets": offsets, "probe": probe}


def reference(traces, alive, offsets, probe):
    signal_traces = traces.astype(jnp.float32)
    spectrum = jnp.fft.fft(signal_traces, axis=1)
    power = jnp.real(spectrum) ** 2 + jnp.imag(spectrum) ** 2
    level = lax.optimization_barrier(jnp.mean(power, axis=1, keepdims=True))
    scale = alive.astype(jnp.float32)[:, None] / jnp.sqrt(power + 0.1 * (level + 1e-05))
    real_part = (jnp.real(spectrum) * scale).astype(jnp.bfloat16)
    imag_part = (jnp.imag(spectrum) * scale).astype(jnp.bfloat16)
    padding = jnp.zeros((WINDOW, NT), jnp.bfloat16)
    real_padded = jnp.concatenate([real_part, padding], axis=0)
    imag_padded = jnp.concatenate([imag_part, padding], axis=0)
    own_real = real_part.astype(jnp.float32)
    own_imag = imag_part.astype(jnp.float32)

    def one_offset(offset):
        start = offset.astype(jnp.int32)
        other_real = lax.dynamic_slice_in_dim(real_padded, start, CHANNELS, 0).astype(jnp.float32)
        other_imag = lax.dynamic_slice_in_dim(imag_padded, start, CHANNELS, 0).astype(jnp.float32)
        cross_real = own_real * other_real + own_imag * other_imag
        cross_imag = own_imag * other_real - own_real * other_imag
        lagged = jnp.fft.ifft(cross_real + 1j * cross_imag, axis=1)
        panel = (jnp.real(lagged) * NT ** 0.5).astype(jnp.bfloat16)
        sketch = jnp.dot(panel.astype(jnp.float32), probe.astype(jnp.float32), preferred_element_type=jnp.float32).astype(jnp.bfloat16)
        sketch_wide_matrix = sketch.astype(jnp.float32)
        gram = jnp.dot(sketch.T.astype(jnp.float32), sketch.astype(jnp.float32), preferred_element_type=jnp.float32)
        moments = jnp.dot(sketch.T.astype(jnp.float32), panel.astype(jnp.float32), preferred_element_type=jnp.float32)
        factor = jnp.linalg.cholesky(gram)
        inverse_transform = jax.scipy.linalg.cho_solve((factor, True), jnp.eye(RANK, dtype=jnp.float32))
        weight_factors = jnp.dot(sketch_wide_matrix, inverse_transform, precision=lax.Precision.HIGHEST)
        cleaned = jnp.dot(weight_factors, moments, precision=lax.Precision.HIGHEST).astype(jnp.bfloat16)
        return (panel, cleaned)
    correlations, denoised = lax.map(one_offset, offsets)
    return (correlations, denoised)
```

```python
import functools
import math

import jax
import jax.numpy as jnp
import numpy as np
from jax import lax
from jax.experimental import pallas as pl
from jax.experimental.pallas import tpu as pltpu
from jax.sharding import PartitionSpec as P

RANK = 64
WINDOW = 256
LANES = 128
ROWS = 16
F32 = jnp.float32
BF16 = jnp.bfloat16
MESH = pl.DeviceIdType.MESH


def tables(total):
    radix = total // LANES
    half = radix // 2 + 1
    n = np.arange(LANES)
    angle = 2.0 * math.pi * ((n[:, None] * n[None, :]) % LANES) / LANES
    cosine, sine = np.cos(angle), np.sin(angle)
    forward = np.block([[cosine, -sine], [sine, cosine]])
    backward = np.block([[cosine, sine], [-sine, cosine]])
    twist = 2.0 * math.pi * np.arange(half)[:, None] * n[None, :] / total
    twists = np.stack([np.cos(twist), np.sin(twist)])[:, :, None, :]
    return (
        jnp.asarray(forward, BF16),
        jnp.asarray(backward, BF16),
        jnp.asarray(twists, F32),
    )


def add(a, b):
    return b if a is None else (a if b is None else a + b)


def sub(a, b):
    if b is None:
        return a
    return -b if a is None else a - b


def turn(value, k, n, sign):
    re, im = value
    if k == 0:
        return value
    c, s = math.cos(2 * math.pi * k / n), sign * math.sin(2 * math.pi * k / n)
    if abs(c) < 1e-12:
        if s > 0:
            return (None if im is None else -im, re)
        return (im, None if re is None else -re)
    if im is None:
        return (re * c, re * s)
    if abs(abs(c) - abs(s)) < 1e-12:
        r = abs(c)
        a, b = math.copysign(1, c), math.copysign(1, s)
        x = (re if a > 0 else -re) - (im if b > 0 else -im)
        y = (re if b > 0 else -re) + (im if a > 0 else -im)
        return (x * r, y * r)
    return (re * c - im * s, re * s + im * c)


def real_forward(x):
    n = len(x)
    if n == 1:
        return [(x[0], None)]
    if n == 2:
        return [(x[0] + x[1], None), (x[0] - x[1], None)]
    even, odd = real_forward(x[0::2]), real_forward(x[1::2])
    out = [None] * (n // 2 + 1)
    for k in range(n // 4 + 1):
        e, o = even[k], turn(odd[k], k, n, -1.0)
        out[k] = (add(e[0], o[0]), add(e[1], o[1]))
        if n // 2 - k != k:
            low = (sub(e[0], o[0]), sub(e[1], o[1]))
            out[n // 2 - k] = (low[0], None if low[1] is None else -low[1])
    return out


def real_backward(v):
    n = 2 * (len(v) - 1)
    if n == 2:
        return [v[0][0] + v[1][0], v[0][0] - v[1][0]]
    even, odd = [], []
    for k in range(n // 4 + 1):
        a, b = v[k], v[n // 2 - k]
        if k == 0:
            even.append((a[0] + b[0], None))
            odd.append((a[0] - b[0], None))
        elif k == n // 4:
            even.append((a[0] + a[0], None))
            odd.append((-(a[1] + a[1]), None))
        else:
            even.append((a[0] + b[0], a[1] - b[1]))
            odd.append(turn((a[0] - b[0], a[1] + b[1]), k, n, 1.0))
    out = [None] * n
    out[0::2] = real_backward(even)
    out[1::2] = real_backward(odd)
    return out


def spectra_kernel(
    peers, chunks, x_ref, alive_ref, forward_ref, twist_ref, slots, turned, level,
    core_s, core_r, z_s, z_r, y_s, y_r, relay_s, relay_r, done_s, done_r,
):
    count, total = x_ref.shape
    radix = total // LANES
    half = radix // 2 + 1
    me = lax.axis_index("fibre")
    core = lax.rem(me, 2)
    chip = me // 2
    odd = lax.rem(chip, 2)
    pair = me + 1 - 2 * core
    across = me + 2 - 4 * odd
    upper, lower = me + 4, me - 4
    has_upper, has_lower = me < peers - 4, me >= 4
    barrier = pltpu.get_barrier_semaphore()
    for peer in (pair, across):
        pl.semaphore_signal(barrier, inc=1, device_id={"fibre": peer}, device_id_type=MESH)

    @pl.when(has_upper)
    def _():
        pl.semaphore_signal(barrier, inc=1, device_id={"fibre": upper}, device_id_type=MESH)

    @pl.when(has_lower)
    def _():
        pl.semaphore_signal(barrier, inc=1, device_id={"fibre": lower}, device_id_type=MESH)

    @pl.loop(0, count // ROWS)
    def _(step):
        rows = pl.ds(pl.multiple_of(step * ROWS, ROWS), ROWS)
        x = [x_ref[rows, a * LANES : (a + 1) * LANES].astype(F32) for a in range(radix)]
        squares = x[0] * x[0]
        for a in range(1, radix):
            squares = squares + x[a] * x[a]
        energy = jnp.sum(squares, axis=1, keepdims=True)
        level[rows, :] = jnp.broadcast_to(0.1 * (energy + 1e-05), (ROWS, LANES))
        for k, (re, im) in enumerate(real_forward(x)):
            cosine, sine = twist_ref[0, k], twist_ref[1, k]
            if im is None:
                turned[k, rows, :LANES] = (re * cosine).astype(BF16)
                turned[k, rows, LANES:] = (-(re * sine)).astype(BF16)
            else:
                turned[k, rows, :LANES] = (re * cosine + im * sine).astype(BF16)
                turned[k, rows, LANES:] = (im * cosine - re * sine).astype(BF16)

    shape = (count, count)
    eye = lax.broadcasted_iota(jnp.int32, shape, 0) == lax.broadcasted_iota(jnp.int32, shape, 1)
    alive = jnp.where(eye, jnp.broadcast_to(alive_ref[...].astype(F32), shape), 0.0)
    alive = jnp.broadcast_to(jnp.sum(alive, axis=1, keepdims=True), (count, LANES))

    met = 2 + has_upper.astype(jnp.int32) + has_lower.astype(jnp.int32)
    pl.semaphore_wait(barrier, met)

    def move(source, target, part, send, recv, index, peer):
        lo, hi = part
        return pltpu.make_async_remote_copy(
            src_ref=slots.at[source, pl.ds(lo, hi - lo)],
            dst_ref=slots.at[target, pl.ds(lo, hi - lo)],
            send_sem=send.at[index],
            recv_sem=recv.at[index],
            device_id={"fibre": peer},
            device_id_type=MESH,
        )

    own, nearer, farther = core, 2 + core, 4 + core
    for index, part in enumerate(chunks):
        for k in range(*part):
            spectrum = jnp.dot(turned[k], forward_ref[...], preferred_element_type=F32)
            re, im = spectrum[:, :LANES], spectrum[:, LANES:]
            scale = alive * lax.rsqrt(re * re + im * im + level[...])
            slots[own, k, :, :LANES] = (re * scale).astype(BF16)
            slots[own, k, :, LANES:] = (im * scale).astype(BF16)

        @pl.when(has_lower)
        def _():
            move(own, farther, part, z_s, z_r, index, lower).start()

        @pl.when(odd == 1)
        def _():
            move(own, nearer, part, y_s, y_r, index, across).start()

        move(own, own, part, core_s, core_r, index, pair).start()

    @pl.when(jnp.logical_not(has_upper))
    def _():
        for k in range(half):
            slots[farther, k] = jnp.zeros((count, 2 * LANES), BF16)

    for index, part in enumerate(chunks):
        @pl.when(has_upper)
        def _():
            move(own, farther, part, z_s, z_r, index, lower).wait_recv()

        @pl.when(odd == 0)
        def _():
            move(farther, nearer, part, y_s, y_r, index, across).start()

        move(farther, farther, part, done_s, done_r, index, pair).start()
        move(own, nearer, part, y_s, y_r, index, across).wait_recv()
        move(nearer, nearer, part, relay_s, relay_r, index, pair).start()
    for index, part in enumerate(chunks):
        move(own, own, part, core_s, core_r, index, pair).wait()
        move(farther, farther, part, done_s, done_r, index, pair).wait()
        move(nearer, nearer, part, relay_s, relay_r, index, pair).wait()
        move(own, nearer, part, y_s, y_r, index, across).wait_send()

        @pl.when(has_lower)
        def _():
            move(own, farther, part, z_s, z_r, index, lower).wait_send()


def spectra(traces, alive, forward, twists, peers):
    count, total = traces.shape
    half = total // LANES // 2 + 1
    pieces = 4
    cuts = [half * i // pieces for i in range(pieces + 1)]
    chunks = tuple(zip(cuts[:-1], cuts[1:]))
    vmem = pl.BlockSpec(memory_space=pltpu.VMEM)
    return pl.pallas_call(
        functools.partial(spectra_kernel, peers, chunks),
        name="spectra",
        out_shape=jax.ShapeDtypeStruct((6, half, count, 2 * LANES), BF16),
        in_specs=[vmem] * 4,
        out_specs=vmem,
        scratch_shapes=[
            pltpu.VMEM((half, count, 2 * LANES), BF16),
            pltpu.VMEM((count, LANES), F32),
        ]
        + [pltpu.SemaphoreType.DMA((pieces,))] * 10,
        compiler_params=pltpu.CompilerParams(collective_id=0, has_side_effects=True),
    )(traces, alive.reshape(1, count), forward, twists)


def panel_kernel(
    offsets_ref, slots, backward_ref, twist_ref, probe_ref, panel_ref, sketch_ref, gram_ref,
    moment_ref, cross, wide,
):
    half, count = slots.shape[1], slots.shape[2]
    radix = 2 * (half - 1)
    total = radix * LANES
    core = lax.rem(lax.axis_index("fibre"), 2)
    start = core * count + offsets_ref[pl.program_id(0)]
    block = start // count
    shift = start - block * count
    after = jnp.minimum(block + 1, 5)
    shape = (count, count)
    gap = lax.broadcasted_iota(jnp.int32, shape, 1) - lax.broadcasted_iota(jnp.int32, shape, 0)
    first = jnp.where(gap == shift, 1.0, 0.0).astype(BF16)
    second = jnp.where(gap == shift - count, 1.0, 0.0).astype(BF16)
    pick = jnp.concatenate([first, second], axis=1)
    for k in range(half):
        both = jnp.concatenate([slots[block, k], slots[after, k]], axis=0)
        other = jnp.dot(pick, both, preferred_element_type=F32)
        own = slots[core, k].astype(F32)
        a, b = own[:, :LANES], own[:, LANES:]
        c, d = other[:, :LANES], other[:, LANES:]
        cross[k, :, :LANES] = (a * c + b * d).astype(BF16)
        cross[k, :, LANES:] = (b * c - a * d).astype(BF16)
    for k in range(half):
        inner = jnp.dot(cross[k], backward_ref[...], preferred_element_type=F32)
        re, im = inner[:, :LANES], inner[:, LANES:]
        cosine, sine = twist_ref[0, k], twist_ref[1, k]
        wide[k, :, :LANES] = re * cosine - im * sine
        if 0 < k < half - 1:
            wide[k, :, LANES:] = re * sine + im * cosine

    @pl.loop(0, count // ROWS)
    def _(step):
        rows = pl.ds(pl.multiple_of(step * ROWS, ROWS), ROWS)
        values = []
        for k in range(half):
            inside = 0 < k < half - 1
            values.append((wide[k, rows, :LANES], wide[k, rows, LANES:] if inside else None))
        for a, out in enumerate(real_backward(values)):
            panel_ref[0, rows, a * LANES : (a + 1) * LANES] = (out * total**-0.5).astype(BF16)

    sketch = jnp.dot(panel_ref[0], probe_ref[...], preferred_element_type=F32)
    flipped = sketch.T.astype(BF16)
    sketch = sketch.astype(BF16)
    sketch_ref[0] = sketch
    gram_ref[0] = jnp.dot(flipped, sketch, preferred_element_type=F32)
    parts, width = moment_ref.shape[1], moment_ref.shape[3]
    for p in range(parts):
        columns = panel_ref[0, :, p * width : (p + 1) * width]
        moment_ref[0, p] = jnp.dot(flipped, columns, preferred_element_type=F32).astype(BF16)


def panels(offsets, slots, backward, twists, probe, peers):
    _, half, count, _ = slots.shape
    total = probe.shape[0]
    many = offsets.shape[0]
    vmem = pl.BlockSpec(memory_space=pltpu.VMEM)
    width = total // peers

    def per(*shape):
        return pl.BlockSpec((1,) + shape, lambda o: (o,) + (0,) * len(shape))

    return pl.pallas_call(
        panel_kernel,
        name="panels",
        grid=(many,),
        out_shape=(
            jax.ShapeDtypeStruct((many, count, total), BF16),
            jax.ShapeDtypeStruct((many, count, RANK), BF16),
            jax.ShapeDtypeStruct((many, RANK, RANK), F32),
            jax.ShapeDtypeStruct((many, peers, RANK, width), BF16),
        ),
        in_specs=[pl.BlockSpec(memory_space=pltpu.SMEM)] + [vmem] * 4,
        out_specs=(per(count, total), per(count, RANK), per(RANK, RANK), per(peers, RANK, width)),
        scratch_shapes=[
            pltpu.VMEM((half, count, 2 * LANES), BF16),
            pltpu.VMEM((half, count, 2 * LANES), F32),
        ],
    )(offsets, slots, backward, twists, probe)


def eliminate(matrix, pivots):
    shape = matrix.shape
    row_at = lax.broadcasted_iota(jnp.int32, shape, 1)
    column_at = lax.broadcasted_iota(jnp.int32, shape, 2)
    for k in pivots:
        row = matrix[:, k : k + 1, :]
        on_column = column_at == k
        column = jnp.sum(jnp.where(on_column, matrix, 0.0), axis=2, keepdims=True)
        pivot = 1.0 / column[:, k : k + 1, :]
        scaled = jnp.where(on_column[:, :1, :], pivot, row * pivot)
        matrix = jnp.where(
            row_at == k, scaled, jnp.where(on_column, 0.0, matrix) - column * scaled
        )
    return matrix


def orders(peers, many):
    bits = [1 << i for i in range(peers.bit_length() - 1)]
    return [bits for _ in range(many)]


def reduce_kernel(
    peers, moment_ref, gram_ref, full, inverse_ref, sums, landed, grams, gram_in,
    rs_s, rs_r, ag_s, ag_r, g_s, g_r,
):
    many = moment_ref.shape[0]
    plan = orders(peers, many)
    steps = len(plan[0])
    me = lax.axis_index("fibre")

    def bit_of(bit):
        return lax.rem(me // bit, 2)

    def partner(bit):
        return me + bit - 2 * bit * bit_of(bit)

    barrier = pltpu.get_barrier_semaphore()
    for bit in plan[0]:
        pl.semaphore_signal(barrier, inc=1, device_id={"fibre": partner(bit)}, device_id_type=MESH)
    pl.semaphore_wait(barrier, steps)

    def remote(src, dst, send, recv, peer):
        return pltpu.make_async_remote_copy(
            src_ref=src, dst_ref=dst, send_sem=send, recv_sem=recv,
            device_id={"fibre": peer}, device_id_type=MESH,
        )

    low = [[0] for _ in range(many)]
    for o in range(many):
        for s in range(steps):
            low[o].append(low[o][s] + bit_of(plan[o][s]) * (peers >> (s + 1)))
    base = [peers - (peers >> s) for s in range(steps)]

    def halve(o, s):
        size = peers >> (s + 1)
        bit = plan[o][s]
        theirs = low[o][s] + (1 - bit_of(bit)) * size
        source = moment_ref if s == 0 else sums
        return remote(
            source.at[o, pl.ds(theirs, size)], landed.at[o, pl.ds(base[s], size)],
            rs_s.at[o, s], rs_r.at[o, s], partner(bit),
        )

    def double(s):
        source = gram_ref if s == 0 else grams.at[s]
        return remote(source, gram_in.at[s], g_s.at[s], g_r.at[s], partner(plan[0][s]))

    def gather(o, s):
        size = peers >> (s + 1)
        here = full.at[o, pl.ds(low[o][s + 1], size)]
        return remote(here, here, ag_s.at[o, s], ag_r.at[o, s], partner(plan[o][s]))

    double(0).start()
    for o in range(many):
        halve(o, 0).start()
    for s in range(steps):
        size = peers >> (s + 1)
        last = s == steps - 1
        double(s).wait_recv()
        before = gram_ref[...] if s == 0 else grams[s]
        total = before + gram_in[s]
        if last:
            matrix = total
        else:
            grams[s + 1] = total
            double(s + 1).start()
        for o in range(many):
            halve(o, s).wait_recv()
            source = moment_ref if s == 0 else sums
            target = full if last else sums
            for p in range(size):
                at = low[o][s + 1] + p
                value = source[o, at].astype(F32) + landed[o, base[s] + p].astype(F32)
                target[o, at] = value.astype(BF16)
            if last:
                gather(o, s).start()
            else:
                halve(o, s + 1).start()
    share = -(-RANK // steps)
    for s in reversed(range(steps)):
        at = (steps - 1 - s) * share
        matrix = eliminate(matrix, range(at, min(at + share, RANK)))
        for o in range(many):
            gather(o, s).wait_recv()
            if s > 0:
                gather(o, s - 1).start()
    inverse_ref[...] = matrix
    for s in range(steps):
        double(s).wait_send()
        for o in range(many):
            halve(o, s).wait_send()
            gather(o, s).wait_send()


def reduced(moments, grams, peers):
    many = moments.shape[0]
    steps = peers.bit_length() - 1
    vmem = pl.BlockSpec(memory_space=pltpu.VMEM)
    dma = pltpu.SemaphoreType.DMA
    return pl.pallas_call(
        functools.partial(reduce_kernel, peers),
        name="reduced",
        out_shape=(
            jax.ShapeDtypeStruct(moments.shape, BF16),
            jax.ShapeDtypeStruct(grams.shape, F32),
        ),
        in_specs=[vmem] * 2,
        out_specs=(vmem, vmem),
        scratch_shapes=[
            pltpu.VMEM(moments.shape, BF16),
            pltpu.VMEM(moments.shape, BF16),
            pltpu.VMEM((steps,) + grams.shape, F32),
            pltpu.VMEM((steps,) + grams.shape, F32),
        ]
        + [dma((many, steps))] * 4
        + [dma((steps,))] * 2,
        compiler_params=pltpu.CompilerParams(collective_id=1, has_side_effects=True),
    )(moments, grams)


def project_kernel(sketch_ref, inverse_ref, moment_ref, out_ref):
    factors = jnp.dot(
        sketch_ref[0].astype(F32), inverse_ref[0],
        precision=lax.Precision.HIGHEST, preferred_element_type=F32,
    ).astype(BF16)
    parts, width = moment_ref.shape[1], moment_ref.shape[3]
    for p in range(parts):
        out_ref[0, :, p * width : (p + 1) * width] = jnp.dot(
            factors, moment_ref[0, p], preferred_element_type=F32
        ).astype(BF16)


def projected(sketches, inverses, moments):
    many, count, _ = sketches.shape
    parts, width = moments.shape[1], moments.shape[3]

    def per(*shape):
        return pl.BlockSpec((1,) + shape, lambda o: (o,) + (0,) * len(shape))

    return pl.pallas_call(
        project_kernel,
        name="projected",
        grid=(many,),
        out_shape=jax.ShapeDtypeStruct((many, count, parts * width), BF16),
        in_specs=[per(count, RANK), per(RANK, RANK), per(parts, RANK, width)],
        out_specs=per(count, parts * width),
    )(sketches, inverses, moments)


def body(traces, alive, offsets, probe):
    peers = lax.axis_size("fibre")
    count, total = traces.shape
    assert WINDOW == 4 * count and peers % 4 == 0
    forward, backward, twists = tables(total)
    slots = spectra(traces, alive, forward, twists, peers)
    correlations, sketches, grams, moments = panels(
        offsets, slots, backward, twists, probe, peers
    )
    moments, inverses = reduced(moments, grams, peers)
    return (correlations, projected(sketches, inverses, moments))


def solution(mesh):
    placed = (P(("groups", "fibre"), None), P(("groups", "fibre")), P(), P())
    return jax.shard_map(
        body,
        mesh=mesh,
        in_specs=placed,
        out_specs=(P(None, ("groups", "fibre"), None), P(None, ("groups", "fibre"), None)),
        check_vma=False,
    )
```

```python
import functools
import math

import jax
import jax.numpy as jnp
import numpy as np
from jax import lax
from jax.experimental import pallas as pl
from jax.experimental.pallas import tpu as pltpu
from jax.sharding import PartitionSpec as P

RANK = 64
WINDOW = 256
LANES = 128
ROWS = 16
SPLIT = 2
OTHERS = (0, 3)
F32 = jnp.float32
BF16 = jnp.bfloat16
MESH = pl.DeviceIdType.MESH


def tables(total):
    radix = total // LANES
    half = radix // 2 + 1
    n = np.arange(LANES)
    angle = 2.0 * math.pi * ((n[:, None] * n[None, :]) % LANES) / LANES
    cosine, sine = np.cos(angle), np.sin(angle)
    forward = np.block([[cosine, -sine], [sine, cosine]])
    backward = np.block([[cosine, sine], [-sine, cosine]])
    twist = 2.0 * math.pi * np.arange(half)[:, None] * n[None, :] / total
    twists = np.stack([np.cos(twist), np.sin(twist)])[:, :, None, :]
    return (
        jnp.asarray(forward, BF16),
        jnp.asarray(backward, BF16),
        jnp.asarray(twists, F32),
    )


def add(a, b):
    return b if a is None else (a if b is None else a + b)


def sub(a, b):
    if b is None:
        return a
    return -b if a is None else a - b


def turn(value, k, n, sign):
    re, im = value
    if k == 0:
        return value
    c, s = math.cos(2 * math.pi * k / n), sign * math.sin(2 * math.pi * k / n)
    if abs(c) < 1e-12:
        if s > 0:
            return (None if im is None else -im, re)
        return (im, None if re is None else -re)
    if im is None:
        return (re * c, re * s)
    if abs(abs(c) - abs(s)) < 1e-12:
        r = abs(c)
        a, b = math.copysign(1, c), math.copysign(1, s)
        x = (re if a > 0 else -re) - (im if b > 0 else -im)
        y = (re if b > 0 else -re) + (im if a > 0 else -im)
        return (x * r, y * r)
    return (re * c - im * s, re * s + im * c)


def real_forward(x):
    n = len(x)
    if n == 1:
        return [(x[0], None)]
    if n == 2:
        return [(x[0] + x[1], None), (x[0] - x[1], None)]
    even, odd = real_forward(x[0::2]), real_forward(x[1::2])
    out = [None] * (n // 2 + 1)
    for k in range(n // 4 + 1):
        e, o = even[k], turn(odd[k], k, n, -1.0)
        out[k] = (add(e[0], o[0]), add(e[1], o[1]))
        if n // 2 - k != k:
            low = (sub(e[0], o[0]), sub(e[1], o[1]))
            out[n // 2 - k] = (low[0], None if low[1] is None else -low[1])
    return out


def real_backward(v):
    n = 2 * (len(v) - 1)
    if n == 2:
        return [v[0][0] + v[1][0], v[0][0] - v[1][0]]
    even, odd = [], []
    for k in range(n // 4 + 1):
        a, b = v[k], v[n // 2 - k]
        if k == 0:
            even.append((a[0] + b[0], None))
            odd.append((a[0] - b[0], None))
        elif k == n // 4:
            even.append((a[0] + a[0], None))
            odd.append((-(a[1] + a[1]), None))
        else:
            even.append((a[0] + b[0], a[1] - b[1]))
            odd.append(turn((a[0] - b[0], a[1] + b[1]), k, n, 1.0))
    out = [None] * n
    out[0::2] = real_backward(even)
    out[1::2] = real_backward(odd)
    return out


def spectra_kernel(
    peers, x_ref, alive_ref, forward_ref, twist_ref, slots, turned, wide,
    core_s, core_r, z_s, z_r, y_s, y_r, relay_s, relay_r, done_s, done_r,
):
    count, total = x_ref.shape
    radix = total // LANES
    half = radix // 2 + 1
    groups = count // ROWS
    me = lax.axis_index("fibre")
    core = lax.rem(me, 2)
    chip = me // 2
    odd = lax.rem(chip, 2)
    pair = me + 1 - 2 * core
    across = me + 2 - 4 * odd
    upper, lower = me + 4, me - 4
    has_upper, has_lower = me < peers - 4, me >= 4
    barrier = pltpu.get_barrier_semaphore()
    for peer in (pair, across):
        pl.semaphore_signal(barrier, inc=1, device_id={"fibre": peer}, device_id_type=MESH)

    @pl.when(has_upper)
    def _():
        pl.semaphore_signal(barrier, inc=1, device_id={"fibre": upper}, device_id_type=MESH)

    @pl.when(has_lower)
    def _():
        pl.semaphore_signal(barrier, inc=1, device_id={"fibre": lower}, device_id_type=MESH)

    shape = (count, count)
    eye = lax.broadcasted_iota(jnp.int32, shape, 0) == lax.broadcasted_iota(jnp.int32, shape, 1)
    alive = jnp.where(eye, jnp.broadcast_to(alive_ref[...].astype(F32), shape), 0.0)
    alive = jnp.broadcast_to(jnp.sum(alive, axis=1, keepdims=True), (count, LANES))

    def move(source, target, send, recv, index, peer):
        return pltpu.make_async_remote_copy(
            src_ref=slots.at[source, index],
            dst_ref=slots.at[target, index],
            send_sem=send.at[index],
            recv_sem=recv.at[index],
            device_id={"fibre": peer},
            device_id_type=MESH,
        )

    own, nearer, farther = core, 2 + core, 4 + core
    for index in range(groups):
        rows = slice(index * ROWS, (index + 1) * ROWS)
        x = [x_ref[rows, a * LANES : (a + 1) * LANES].astype(F32) for a in range(radix)]
        squares = x[0] * x[0]
        for a in range(1, radix):
            squares = squares + x[a] * x[a]
        energy = jnp.sum(squares, axis=1, keepdims=True)
        level = jnp.broadcast_to(0.1 * (energy + 1e-05), (ROWS, LANES))
        for k, (re, im) in enumerate(real_forward(x)):
            cosine, sine = twist_ref[0, k], twist_ref[1, k]
            if im is None:
                turned[k, :, :LANES] = (re * cosine).astype(BF16)
                turned[k, :, LANES:] = (-(re * sine)).astype(BF16)
            else:
                turned[k, :, :LANES] = (re * cosine + im * sine).astype(BF16)
                turned[k, :, LANES:] = (im * cosine - re * sine).astype(BF16)
        stacked = turned[...].reshape(half * ROWS, 2 * LANES)
        wide[...] = jnp.dot(stacked, forward_ref[...], preferred_element_type=F32)
        for k in range(half):
            at = slice(k * ROWS, (k + 1) * ROWS)
            re, im = wide[at, :LANES], wide[at, LANES:]
            scale = alive[rows] * lax.rsqrt(re * re + im * im + level)
            slots[own, index, k, :, :LANES] = (re * scale).astype(BF16)
            slots[own, index, k, :, LANES:] = (im * scale).astype(BF16)
        if index == 0:
            met = 2 + has_upper.astype(jnp.int32) + has_lower.astype(jnp.int32)
            pl.semaphore_wait(barrier, met)

        @pl.when(has_lower)
        def _():
            move(own, farther, z_s, z_r, index, lower).start()

        @pl.when(odd == 1)
        def _():
            move(own, nearer, y_s, y_r, index, across).start()

        move(own, own, core_s, core_r, index, pair).start()

    @pl.when(jnp.logical_not(has_upper))
    def _():
        for index in range(groups):
            for k in range(half):
                slots[farther, index, k] = jnp.zeros((ROWS, 2 * LANES), BF16)

    for index in range(groups):
        @pl.when(has_upper)
        def _():
            move(own, farther, z_s, z_r, index, lower).wait_recv()

        @pl.when(odd == 0)
        def _():
            move(farther, nearer, y_s, y_r, index, across).start()

        move(farther, farther, done_s, done_r, index, pair).start()
        move(own, nearer, y_s, y_r, index, across).wait_recv()
        move(nearer, nearer, relay_s, relay_r, index, pair).start()
    for index in range(groups):
        move(own, own, core_s, core_r, index, pair).wait()
        move(farther, farther, done_s, done_r, index, pair).wait()
        move(nearer, nearer, relay_s, relay_r, index, pair).wait()
        move(own, nearer, y_s, y_r, index, across).wait_send()

        @pl.when(has_lower)
        def _():
            move(own, farther, z_s, z_r, index, lower).wait_send()


def spectra(traces, alive, forward, twists, peers):
    count, total = traces.shape
    half = total // LANES // 2 + 1
    groups = count // ROWS
    vmem = pl.BlockSpec(memory_space=pltpu.VMEM)
    return pl.pallas_call(
        functools.partial(spectra_kernel, peers),
        name="spectra",
        out_shape=jax.ShapeDtypeStruct((6, groups, half, ROWS, 2 * LANES), BF16),
        in_specs=[vmem] * 4,
        out_specs=vmem,
        scratch_shapes=[
            pltpu.VMEM((half, ROWS, 2 * LANES), BF16),
            pltpu.VMEM((half * ROWS, 2 * LANES), F32),
        ]
        + [pltpu.SemaphoreType.DMA((groups,))] * 10,
        compiler_params=pltpu.CompilerParams(collective_id=0, has_side_effects=True),
    )(traces, alive.reshape(1, count), forward, twists)


def panel_kernel(
    offsets_ref, slots, backward_ref, twist_ref, probe_ref, panel_ref, sketch_ref, gram_ref,
    moment_ref, cross, inner, wide,
):
    half, count = slots.shape[2], slots.shape[1] * slots.shape[3]
    radix = 2 * (half - 1)
    total = radix * LANES
    core = lax.rem(lax.axis_index("fibre"), 2)
    start = core * count + offsets_ref[pl.program_id(0)]
    block = start // count
    shift = start - block * count
    after = jnp.minimum(block + 1, 5)
    shape = (count, count)
    gap = lax.broadcasted_iota(jnp.int32, shape, 1) - lax.broadcasted_iota(jnp.int32, shape, 0)
    first = jnp.where(gap == shift, 1.0, 0.0).astype(BF16)
    second = jnp.where(gap == shift - count, 1.0, 0.0).astype(BF16)
    pick = jnp.concatenate([first, second], axis=1)
    for k in range(half):
        flat = (count, 2 * LANES)
        both = [slots[block, :, k].reshape(flat), slots[after, :, k].reshape(flat)]
        both = jnp.concatenate(both, axis=0)
        other = jnp.dot(pick, both, preferred_element_type=F32)
        own = slots[core, :, k].reshape(flat).astype(F32)
        a, b = own[:, :LANES], own[:, LANES:]
        c, d = other[:, :LANES], other[:, LANES:]
        cross[k, :, :LANES] = (a * c + b * d).astype(BF16)
        cross[k, :, LANES:] = (b * c - a * d).astype(BF16)
    stacked = cross[...].reshape(half * count, 2 * LANES)
    inner[...] = jnp.dot(stacked, backward_ref[...], preferred_element_type=F32)
    for k in range(half):
        at = slice(k * count, (k + 1) * count)
        re, im = inner[at, :LANES], inner[at, LANES:]
        cosine, sine = twist_ref[0, k], twist_ref[1, k]
        wide[k, :, :LANES] = re * cosine - im * sine
        if 0 < k < half - 1:
            wide[k, :, LANES:] = re * sine + im * cosine

    @pl.loop(0, count // ROWS)
    def _(step):
        rows = pl.ds(pl.multiple_of(step * ROWS, ROWS), ROWS)
        values = []
        for k in range(half):
            inside = 0 < k < half - 1
            values.append((wide[k, rows, :LANES], wide[k, rows, LANES:] if inside else None))
        for a, out in enumerate(real_backward(values)):
            panel_ref[0, rows, a * LANES : (a + 1) * LANES] = (out * total**-0.5).astype(BF16)

    sketch = lax.dot_general(
        panel_ref[0], probe_ref[...], (((1,), (1,)), ((), ())), preferred_element_type=F32
    )
    flipped = sketch.T.astype(BF16)
    sketch = sketch.astype(BF16)
    sketch_ref[0] = sketch
    gram_ref[0] = jnp.dot(flipped, sketch, preferred_element_type=F32)
    split, parts, tall, width = moment_ref.shape
    for p in range(parts):
        columns = panel_ref[0, :, p * width : (p + 1) * width]
        moments = jnp.dot(flipped, columns, preferred_element_type=F32).astype(BF16)
        for h in range(split):
            moment_ref[h, p] = moments[h * tall : (h + 1) * tall]


def panels(offsets, slots, backward, twists, probe, peers):
    _, groups, half, rows, _ = slots.shape
    count = groups * rows
    total = probe.shape[1]
    many = offsets.shape[0]
    vmem = pl.BlockSpec(memory_space=pltpu.VMEM)
    width = total // peers

    def per(*shape):
        return pl.BlockSpec((1,) + shape, lambda o: (o,) + (0,) * len(shape))

    return pl.pallas_call(
        panel_kernel,
        name="panels",
        grid=(many,),
        out_shape=(
            jax.ShapeDtypeStruct((many, count, total), BF16),
            jax.ShapeDtypeStruct((many, count, RANK), BF16),
            jax.ShapeDtypeStruct((many, RANK, RANK), F32),
            jax.ShapeDtypeStruct((many * SPLIT, peers, RANK // SPLIT, width), BF16),
        ),
        in_specs=[pl.BlockSpec(memory_space=pltpu.SMEM)] + [vmem] * 4,
        out_specs=(
            per(count, total), per(count, RANK), per(RANK, RANK),
            pl.BlockSpec((SPLIT, peers, RANK // SPLIT, width), lambda o: (o, 0, 0, 0)),
        ),
        scratch_shapes=[
            pltpu.VMEM((half, count, 2 * LANES), BF16),
            pltpu.VMEM((half * count, 2 * LANES), F32),
            pltpu.VMEM((half, count, 2 * LANES), F32),
        ],
    )(offsets, slots, backward, twists, probe)


def eliminate(matrix, pivots):
    shape = matrix.shape
    row_at = lax.broadcasted_iota(jnp.int32, shape, 1)
    column_at = lax.broadcasted_iota(jnp.int32, shape, 2)
    for k in pivots:
        row = matrix[:, k : k + 1, :]
        on_column = column_at == k
        column = jnp.sum(jnp.where(on_column, matrix, 0.0), axis=2, keepdims=True)
        pivot = 1.0 / column[:, k : k + 1, :]
        scaled = jnp.where(on_column[:, :1, :], pivot, row * pivot)
        matrix = jnp.where(
            row_at == k, scaled, jnp.where(on_column, 0.0, matrix) - column * scaled
        )
    return matrix


def orders(peers, many):
    bits = [1 << i for i in range(peers.bit_length() - 1)]
    other = bits[:1] + bits[2:] + bits[1:2]
    return [other if o in OTHERS else bits for o in range(many)]


def reduce_kernel(
    peers, moment_ref, gram_ref, full, inverse_ref, sums, landed, grams, gram_in,
    rs_s, rs_r, ag_s, ag_r, g_s, g_r,
):
    many = moment_ref.shape[0]
    plan = orders(peers, many)
    steps = len(plan[0])
    me = lax.axis_index("fibre")

    def bit_of(bit):
        return lax.rem(me // bit, 2)

    def partner(bit):
        return me + bit - 2 * bit * bit_of(bit)

    several = gram_ref.shape[0]
    tall = several * RANK
    loose = gram_ref[...].reshape(tall, RANK)
    grams[0] = jnp.concatenate([loose[: tall // 2], loose[tall // 2 :]], axis=1)
    barrier = pltpu.get_barrier_semaphore()
    for bit in plan[0]:
        pl.semaphore_signal(barrier, inc=1, device_id={"fibre": partner(bit)}, device_id_type=MESH)
    pl.semaphore_wait(barrier, steps)

    def remote(src, dst, send, recv, peer):
        return pltpu.make_async_remote_copy(
            src_ref=src, dst_ref=dst, send_sem=send, recv_sem=recv,
            device_id={"fibre": peer}, device_id_type=MESH,
        )

    low = [[0] for _ in range(many)]
    for o in range(many):
        for s in range(steps):
            low[o].append(low[o][s] + bit_of(plan[o][s]) * (peers >> (s + 1)))
    base = [peers - (peers >> s) for s in range(steps)]

    def halve(o, s):
        size = peers >> (s + 1)
        bit = plan[o][s]
        theirs = low[o][s] + (1 - bit_of(bit)) * size
        source = moment_ref if s == 0 else sums
        return remote(
            source.at[o, pl.ds(theirs, size)], landed.at[o, pl.ds(base[s], size)],
            rs_s.at[o, s], rs_r.at[o, s], partner(bit),
        )

    def double(s):
        return remote(grams.at[s], gram_in.at[s], g_s.at[s], g_r.at[s], partner(plan[0][s]))

    def gather(o, s):
        size = peers >> (s + 1)
        here = full.at[o, pl.ds(low[o][s + 1], size)]
        return remote(here, here, ag_s.at[o, s], ag_r.at[o, s], partner(plan[o][s]))

    for o in range(many):
        halve(o, 0).start()
    double(0).start()
    for s in range(steps):
        size = peers >> (s + 1)
        last = s == steps - 1
        for o in range(many):
            halve(o, s).wait_recv()
            source = moment_ref if s == 0 else sums
            target = full if last else sums
            for p in range(size):
                at = low[o][s + 1] + p
                value = source[o, at].astype(F32) + landed[o, base[s] + p].astype(F32)
                target[o, at] = value.astype(BF16)
            if last:
                gather(o, s).start()
            else:
                halve(o, s + 1).start()
        double(s).wait_recv()
        total = grams[s] + gram_in[s]
        if last:
            loose = jnp.concatenate([total[:, :RANK], total[:, RANK:]], axis=0)
            matrix = loose.reshape(several, RANK, RANK)
        else:
            grams[s + 1] = total
            double(s + 1).start()
    share = -(-RANK // steps)
    for s in reversed(range(steps)):
        at = (steps - 1 - s) * share
        matrix = eliminate(matrix, range(at, min(at + share, RANK)))
        for o in range(many):
            gather(o, s).wait_recv()
            if s > 0:
                gather(o, s - 1).start()
    inverse_ref[...] = matrix
    for s in range(steps):
        double(s).wait_send()
        for o in range(many):
            halve(o, s).wait_send()
            gather(o, s).wait_send()


def reduced(moments, grams, peers):
    many = moments.shape[0]
    steps = peers.bit_length() - 1
    vmem = pl.BlockSpec(memory_space=pltpu.VMEM)
    dma = pltpu.SemaphoreType.DMA
    return pl.pallas_call(
        functools.partial(reduce_kernel, peers),
        name="reduced",
        out_shape=(
            jax.ShapeDtypeStruct(moments.shape, BF16),
            jax.ShapeDtypeStruct(grams.shape, F32),
        ),
        in_specs=[vmem] * 2,
        out_specs=(vmem, vmem),
        scratch_shapes=[
            pltpu.VMEM(moments.shape, BF16),
            pltpu.VMEM(moments.shape, BF16),
            pltpu.VMEM((steps, grams.shape[0] * RANK // 2, 2 * RANK), F32),
            pltpu.VMEM((steps, grams.shape[0] * RANK // 2, 2 * RANK), F32),
        ]
        + [dma((many, steps))] * 4
        + [dma((steps,))] * 2,
        compiler_params=pltpu.CompilerParams(collective_id=1, has_side_effects=True),
    )(moments, grams)


def project_kernel(sketch_ref, inverse_ref, moment_ref, out_ref):
    factors = jnp.dot(
        sketch_ref[0].astype(F32), inverse_ref[0],
        precision=lax.Precision.HIGHEST, preferred_element_type=F32,
    ).astype(BF16)
    _, parts, _, width = moment_ref.shape
    for p in range(parts):
        out_ref[0, :, p * width : (p + 1) * width] = jnp.dot(
            factors, moment_ref[:, p].reshape(RANK, width), preferred_element_type=F32
        ).astype(BF16)


def projected(sketches, inverses, moments):
    many, count, _ = sketches.shape
    parts, width = moments.shape[1], moments.shape[3]

    def per(*shape):
        return pl.BlockSpec((1,) + shape, lambda o: (o,) + (0,) * len(shape))

    return pl.pallas_call(
        project_kernel,
        name="projected",
        grid=(many,),
        out_shape=jax.ShapeDtypeStruct((many, count, parts * width), BF16),
        in_specs=[
            per(count, RANK), per(RANK, RANK),
            pl.BlockSpec((SPLIT, parts, RANK // SPLIT, width), lambda o: (o, 0, 0, 0)),
        ],
        out_specs=per(count, parts * width),
    )(sketches, inverses, moments)


def body(traces, alive, offsets, probe):
    peers = lax.axis_size("fibre")
    count, total = traces.shape
    assert WINDOW == 4 * count and peers % 4 == 0
    forward, backward, twists = tables(total)
    slots = spectra(traces, alive, forward, twists, peers)
    correlations, sketches, grams, moments = panels(
        offsets, slots, backward, twists, probe.T, peers
    )
    moments, inverses = reduced(moments, grams, peers)
    return (correlations, projected(sketches, inverses, moments))


def solution(mesh):
    placed = (P(("groups", "fibre"), None), P(("groups", "fibre")), P(), P())
    return jax.shard_map(
        body,
        mesh=mesh,
        in_specs=placed,
        out_specs=(P(None, ("groups", "fibre"), None), P(None, ("groups", "fibre"), None)),
        check_vma=False,
    )
```

```python
import functools
import math

import jax
import jax.numpy as jnp
import numpy as np
from jax import lax
from jax.experimental import pallas as pl
from jax.experimental.pallas import tpu as pltpu
from jax.sharding import PartitionSpec as P

RANK = 64
WINDOW = 256
LANES = 128
ROWS = 16
SPLIT = 2
OTHERS = (0, 3)
F32 = jnp.float32
BF16 = jnp.bfloat16
MESH = pl.DeviceIdType.MESH


def tables(total):
    radix = total // LANES
    half = radix // 2 + 1
    n = np.arange(LANES)
    angle = 2.0 * math.pi * ((n[:, None] * n[None, :]) % LANES) / LANES
    cosine, sine = np.cos(angle), np.sin(angle)
    forward = np.block([[cosine, -sine], [sine, cosine]])
    backward = np.block([[cosine, sine], [-sine, cosine]])
    twist = 2.0 * math.pi * np.arange(half)[:, None] * n[None, :] / total
    twists = np.stack([np.cos(twist), np.sin(twist)])[:, :, None, :]
    return (
        jnp.asarray(forward, BF16),
        jnp.asarray(backward, BF16),
        jnp.asarray(twists, F32),
    )


def add(a, b):
    return b if a is None else (a if b is None else a + b)


def sub(a, b):
    if b is None:
        return a
    return -b if a is None else a - b


def turn(value, k, n, sign):
    re, im = value
    if k == 0:
        return value
    c, s = math.cos(2 * math.pi * k / n), sign * math.sin(2 * math.pi * k / n)
    if abs(c) < 1e-12:
        if s > 0:
            return (None if im is None else -im, re)
        return (im, None if re is None else -re)
    if im is None:
        return (re * c, re * s)
    if abs(abs(c) - abs(s)) < 1e-12:
        r = abs(c)
        a, b = math.copysign(1, c), math.copysign(1, s)
        x = (re if a > 0 else -re) - (im if b > 0 else -im)
        y = (re if b > 0 else -re) + (im if a > 0 else -im)
        return (x * r, y * r)
    return (re * c - im * s, re * s + im * c)


def real_forward(x):
    n = len(x)
    if n == 1:
        return [(x[0], None)]
    if n == 2:
        return [(x[0] + x[1], None), (x[0] - x[1], None)]
    even, odd = real_forward(x[0::2]), real_forward(x[1::2])
    out = [None] * (n // 2 + 1)
    for k in range(n // 4 + 1):
        e, o = even[k], turn(odd[k], k, n, -1.0)
        out[k] = (add(e[0], o[0]), add(e[1], o[1]))
        if n // 2 - k != k:
            low = (sub(e[0], o[0]), sub(e[1], o[1]))
            out[n // 2 - k] = (low[0], None if low[1] is None else -low[1])
    return out


def real_backward(v):
    n = 2 * (len(v) - 1)
    if n == 2:
        return [v[0][0] + v[1][0], v[0][0] - v[1][0]]
    even, odd = [], []
    for k in range(n // 4 + 1):
        a, b = v[k], v[n // 2 - k]
        if k == 0:
            even.append((a[0] + b[0], None))
            odd.append((a[0] - b[0], None))
        elif k == n // 4:
            even.append((a[0] + a[0], None))
            odd.append((-(a[1] + a[1]), None))
        else:
            even.append((a[0] + b[0], a[1] - b[1]))
            odd.append(turn((a[0] - b[0], a[1] + b[1]), k, n, 1.0))
    out = [None] * n
    out[0::2] = real_backward(even)
    out[1::2] = real_backward(odd)
    return out


def spectra_kernel(
    peers, x_ref, alive_ref, forward_ref, twist_ref, slots, turned, wide,
    core_s, core_r, z_s, z_r, y_s, y_r, relay_s, relay_r, done_s, done_r,
):
    count, total = x_ref.shape
    radix = total // LANES
    half = radix // 2 + 1
    groups = count // ROWS
    me = lax.axis_index("fibre")
    core = lax.rem(me, 2)
    chip = me // 2
    odd = lax.rem(chip, 2)
    pair = me + 1 - 2 * core
    across = me + 2 - 4 * odd
    upper, lower = me + 4, me - 4
    has_upper, has_lower = me < peers - 4, me >= 4
    barrier = pltpu.get_barrier_semaphore()
    for peer in (pair, across):
        pl.semaphore_signal(barrier, inc=1, device_id={"fibre": peer}, device_id_type=MESH)

    @pl.when(has_upper)
    def _():
        pl.semaphore_signal(barrier, inc=1, device_id={"fibre": upper}, device_id_type=MESH)

    @pl.when(has_lower)
    def _():
        pl.semaphore_signal(barrier, inc=1, device_id={"fibre": lower}, device_id_type=MESH)

    shape = (count, count)
    eye = lax.broadcasted_iota(jnp.int32, shape, 0) == lax.broadcasted_iota(jnp.int32, shape, 1)
    alive = jnp.where(eye, jnp.broadcast_to(alive_ref[...].astype(F32), shape), 0.0)
    alive = jnp.broadcast_to(jnp.sum(alive, axis=1, keepdims=True), (count, LANES))

    def move(source, target, send, recv, index, peer):
        return pltpu.make_async_remote_copy(
            src_ref=slots.at[source, index],
            dst_ref=slots.at[target, index],
            send_sem=send.at[index],
            recv_sem=recv.at[index],
            device_id={"fibre": peer},
            device_id_type=MESH,
        )

    own, nearer, farther = core, 2 + core, 4 + core
    for index in range(groups):
        rows = slice(index * ROWS, (index + 1) * ROWS)
        x = [x_ref[rows, a * LANES : (a + 1) * LANES].astype(F32) for a in range(radix)]
        squares = x[0] * x[0]
        for a in range(1, radix):
            squares = squares + x[a] * x[a]
        energy = jnp.sum(squares, axis=1, keepdims=True)
        level = jnp.broadcast_to(0.1 * (energy + 1e-05), (ROWS, LANES))
        for k, (re, im) in enumerate(real_forward(x)):
            cosine, sine = twist_ref[0, k], twist_ref[1, k]
            if im is None:
                turned[k, :, :LANES] = (re * cosine).astype(BF16)
                turned[k, :, LANES:] = (-(re * sine)).astype(BF16)
            else:
                turned[k, :, :LANES] = (re * cosine + im * sine).astype(BF16)
                turned[k, :, LANES:] = (im * cosine - re * sine).astype(BF16)
        stacked = turned[...].reshape(half * ROWS, 2 * LANES)
        wide[...] = jnp.dot(stacked, forward_ref[...], preferred_element_type=F32)
        for k in range(half):
            at = slice(k * ROWS, (k + 1) * ROWS)
            re, im = wide[at, :LANES], wide[at, LANES:]
            scale = alive[rows] * lax.rsqrt(re * re + im * im + level)
            slots[own, index, k, :, :LANES] = (re * scale).astype(BF16)
            slots[own, index, k, :, LANES:] = (im * scale).astype(BF16)
        if index == 0:
            met = 2 + has_upper.astype(jnp.int32) + has_lower.astype(jnp.int32)
            pl.semaphore_wait(barrier, met)

        @pl.when(has_lower)
        def _():
            move(own, farther, z_s, z_r, index, lower).start()

        @pl.when(odd == 1)
        def _():
            move(own, nearer, y_s, y_r, index, across).start()

        move(own, own, core_s, core_r, index, pair).start()

    @pl.when(jnp.logical_not(has_upper))
    def _():
        for index in range(groups):
            for k in range(half):
                slots[farther, index, k] = jnp.zeros((ROWS, 2 * LANES), BF16)

    for index in range(groups):
        @pl.when(has_upper)
        def _():
            move(own, farther, z_s, z_r, index, lower).wait_recv()

        @pl.when(odd == 0)
        def _():
            move(farther, nearer, y_s, y_r, index, across).start()

        move(farther, farther, done_s, done_r, index, pair).start()
        move(own, nearer, y_s, y_r, index, across).wait_recv()
        move(nearer, nearer, relay_s, relay_r, index, pair).start()
    for index in range(groups):
        move(own, own, core_s, core_r, index, pair).wait()
        move(farther, farther, done_s, done_r, index, pair).wait()
        move(nearer, nearer, relay_s, relay_r, index, pair).wait()
        move(own, nearer, y_s, y_r, index, across).wait_send()

        @pl.when(has_lower)
        def _():
            move(own, farther, z_s, z_r, index, lower).wait_send()


def spectra(traces, alive, forward, twists, peers):
    count, total = traces.shape
    half = total // LANES // 2 + 1
    groups = count // ROWS
    vmem = pl.BlockSpec(memory_space=pltpu.VMEM)
    return pl.pallas_call(
        functools.partial(spectra_kernel, peers),
        name="spectra",
        out_shape=jax.ShapeDtypeStruct((6, groups, half, ROWS, 2 * LANES), BF16),
        in_specs=[vmem] * 4,
        out_specs=vmem,
        scratch_shapes=[
            pltpu.VMEM((half, ROWS, 2 * LANES), BF16),
            pltpu.VMEM((half * ROWS, 2 * LANES), F32),
        ]
        + [pltpu.SemaphoreType.DMA((groups,))] * 10,
        compiler_params=pltpu.CompilerParams(collective_id=0, has_side_effects=True),
    )(traces, alive.reshape(1, count), forward, twists)


def make_panel(
    o, offsets_ref, slots, backward_ref, twist_ref, probe_ref, panel_ref, sketch_ref,
    moment_ref, cross, inner, wide,
):
    half, count = slots.shape[2], slots.shape[1] * slots.shape[3]
    radix = 2 * (half - 1)
    total = radix * LANES
    core = lax.rem(lax.axis_index("fibre"), 2)
    start = core * count + offsets_ref[o]
    block = start // count
    shift = start - block * count
    after = jnp.minimum(block + 1, 5)
    shape = (count, count)
    gap = lax.broadcasted_iota(jnp.int32, shape, 1) - lax.broadcasted_iota(jnp.int32, shape, 0)
    first = jnp.where(gap == shift, 1.0, 0.0).astype(BF16)
    second = jnp.where(gap == shift - count, 1.0, 0.0).astype(BF16)
    pick = jnp.concatenate([first, second], axis=1)
    for k in range(half):
        flat = (count, 2 * LANES)
        both = [slots[block, :, k].reshape(flat), slots[after, :, k].reshape(flat)]
        both = jnp.concatenate(both, axis=0)
        other = jnp.dot(pick, both, preferred_element_type=F32)
        own = slots[core, :, k].reshape(flat).astype(F32)
        a, b = own[:, :LANES], own[:, LANES:]
        c, d = other[:, :LANES], other[:, LANES:]
        cross[k, :, :LANES] = (a * c + b * d).astype(BF16)
        cross[k, :, LANES:] = (b * c - a * d).astype(BF16)
    stacked = cross[...].reshape(half * count, 2 * LANES)
    inner[...] = jnp.dot(stacked, backward_ref[...], preferred_element_type=F32)
    for k in range(half):
        at = slice(k * count, (k + 1) * count)
        re, im = inner[at, :LANES], inner[at, LANES:]
        cosine, sine = twist_ref[0, k], twist_ref[1, k]
        wide[k, :, :LANES] = re * cosine - im * sine
        if 0 < k < half - 1:
            wide[k, :, LANES:] = re * sine + im * cosine

    @pl.loop(0, count // ROWS)
    def _(step):
        rows = pl.ds(pl.multiple_of(step * ROWS, ROWS), ROWS)
        values = []
        for k in range(half):
            inside = 0 < k < half - 1
            values.append((wide[k, rows, :LANES], wide[k, rows, LANES:] if inside else None))
        for a, out in enumerate(real_backward(values)):
            panel_ref[o, rows, a * LANES : (a + 1) * LANES] = (out * total**-0.5).astype(BF16)

    sketch = lax.dot_general(
        panel_ref[o], probe_ref[...], (((1,), (1,)), ((), ())), preferred_element_type=F32
    )
    flipped = sketch.T.astype(BF16)
    sketch = sketch.astype(BF16)
    sketch_ref[o] = sketch
    gram = jnp.dot(flipped, sketch, preferred_element_type=F32)
    parts, tall, width = moment_ref.shape[1:]
    split = RANK // tall
    for p in range(parts):
        columns = panel_ref[o, :, p * width : (p + 1) * width]
        moments = jnp.dot(flipped, columns, preferred_element_type=F32).astype(BF16)
        for h in range(split):
            moment_ref[o * split + h, p] = moments[h * tall : (h + 1) * tall]
    return gram


def eliminate(matrix, pivots):
    shape = matrix.shape
    row_at = lax.broadcasted_iota(jnp.int32, shape, 1)
    column_at = lax.broadcasted_iota(jnp.int32, shape, 2)
    for k in pivots:
        row = matrix[:, k : k + 1, :]
        on_column = column_at == k
        column = jnp.sum(jnp.where(on_column, matrix, 0.0), axis=2, keepdims=True)
        pivot = 1.0 / column[:, k : k + 1, :]
        scaled = jnp.where(on_column[:, :1, :], pivot, row * pivot)
        matrix = jnp.where(
            row_at == k, scaled, jnp.where(on_column, 0.0, matrix) - column * scaled
        )
    return matrix


def orders(peers, many):
    bits = [1 << i for i in range(peers.bit_length() - 1)]
    other = bits[:1] + bits[2:] + bits[1:2]
    return [other if o in OTHERS else bits for o in range(many)]


def reduce_kernel(
    peers, offsets_ref, slots, backward_ref, twist_ref, probe_ref, panel_ref, sketch_ref, full,
    inverse_ref, cross, inner, wide, moment_ref, sums, landed, grams, gram_in,
    rs_s, rs_r, ag_s, ag_r, g_s, g_r,
):
    many = moment_ref.shape[0]
    plan = orders(peers, many)
    steps = len(plan[0])
    me = lax.axis_index("fibre")

    def bit_of(bit):
        return lax.rem(me // bit, 2)

    def partner(bit):
        return me + bit - 2 * bit * bit_of(bit)

    several = panel_ref.shape[0]
    barrier = pltpu.get_barrier_semaphore()
    for bit in plan[0]:
        pl.semaphore_signal(barrier, inc=1, device_id={"fibre": partner(bit)}, device_id_type=MESH)

    def remote(src, dst, send, recv, peer):
        return pltpu.make_async_remote_copy(
            src_ref=src, dst_ref=dst, send_sem=send, recv_sem=recv,
            device_id={"fibre": peer}, device_id_type=MESH,
        )

    low = [[0] for _ in range(many)]
    for o in range(many):
        for s in range(steps):
            low[o].append(low[o][s] + bit_of(plan[o][s]) * (peers >> (s + 1)))
    base = [peers - (peers >> s) for s in range(steps)]

    def halve(o, s):
        size = peers >> (s + 1)
        bit = plan[o][s]
        theirs = low[o][s] + (1 - bit_of(bit)) * size
        source = moment_ref if s == 0 else sums
        return remote(
            source.at[o, pl.ds(theirs, size)], landed.at[o, pl.ds(base[s], size)],
            rs_s.at[o, s], rs_r.at[o, s], partner(bit),
        )

    def double(s):
        return remote(grams.at[s], gram_in.at[s], g_s.at[s], g_r.at[s], partner(plan[0][s]))

    def gather(o, s):
        size = peers >> (s + 1)
        here = full.at[o, pl.ds(low[o][s + 1], size)]
        return remote(here, here, ag_s.at[o, s], ag_r.at[o, s], partner(plan[o][s]))

    def advance(o, s):
        size = peers >> (s + 1)
        last = s == steps - 1
        halve(o, s).wait_recv()
        source = moment_ref if s == 0 else sums
        target = full if last else sums
        for p in range(size):
            at = low[o][s + 1] + p
            value = source[o, at].astype(F32) + landed[o, base[s] + p].astype(F32)
            target[o, at] = value.astype(BF16)
        if last:
            gather(o, s).start()
        else:
            halve(o, s + 1).start()

    split = many // several
    reached = [0] * many
    loose = []
    for panel in range(several):
        loose.append(
            make_panel(
                panel, offsets_ref, slots, backward_ref, twist_ref, probe_ref, panel_ref,
                sketch_ref, moment_ref, cross, inner, wide,
            )
        )
        if panel == 0:
            pl.semaphore_wait(barrier, steps)
        for o in range(panel * split, (panel + 1) * split):
            halve(o, 0).start()
        if panel == several - 1:
            loose = jnp.concatenate(loose, axis=0)
            tall = several * RANK
            grams[0] = jnp.concatenate([loose[: tall // 2], loose[tall // 2 :]], axis=1)
            double(0).start()
        for o in range(panel * split):
            if reached[o] < steps - 1:
                advance(o, reached[o])
                reached[o] += 1
    for s in range(steps):
        last = s == steps - 1
        for o in range(many):
            if reached[o] == s:
                advance(o, s)
                reached[o] += 1
        double(s).wait_recv()
        total = grams[s] + gram_in[s]
        if last:
            loose = jnp.concatenate([total[:, :RANK], total[:, RANK:]], axis=0)
            matrix = loose.reshape(several, RANK, RANK)
        else:
            grams[s + 1] = total
            double(s + 1).start()
    share = -(-RANK // steps)
    for s in reversed(range(steps)):
        at = (steps - 1 - s) * share
        matrix = eliminate(matrix, range(at, min(at + share, RANK)))
        for o in range(many):
            gather(o, s).wait_recv()
            if s > 0:
                gather(o, s - 1).start()
    inverse_ref[...] = matrix
    for s in range(steps):
        double(s).wait_send()
        for o in range(many):
            halve(o, s).wait_send()
            gather(o, s).wait_send()


def reduced(offsets, slots, backward, twists, probe, peers):
    _, groups, half, rows, _ = slots.shape
    count = groups * rows
    total = probe.shape[1]
    several = offsets.shape[0]
    many = several * SPLIT
    steps = peers.bit_length() - 1
    moments = (many, peers, RANK // SPLIT, total // peers)
    packed = (steps, several * RANK // 2, 2 * RANK)
    vmem = pl.BlockSpec(memory_space=pltpu.VMEM)
    dma = pltpu.SemaphoreType.DMA
    return pl.pallas_call(
        functools.partial(reduce_kernel, peers),
        name="reduced",
        out_shape=(
            jax.ShapeDtypeStruct((several, count, total), BF16),
            jax.ShapeDtypeStruct((several, count, RANK), BF16),
            jax.ShapeDtypeStruct(moments, BF16),
            jax.ShapeDtypeStruct((several, RANK, RANK), F32),
        ),
        in_specs=[pl.BlockSpec(memory_space=pltpu.SMEM)] + [vmem] * 4,
        out_specs=(vmem,) * 4,
        scratch_shapes=[
            pltpu.VMEM((half, count, 2 * LANES), BF16),
            pltpu.VMEM((half * count, 2 * LANES), F32),
            pltpu.VMEM((half, count, 2 * LANES), F32),
            pltpu.VMEM(moments, BF16),
            pltpu.VMEM(moments, BF16),
            pltpu.VMEM(moments, BF16),
            pltpu.VMEM(packed, F32),
            pltpu.VMEM(packed, F32),
        ]
        + [dma((many, steps))] * 4
        + [dma((steps,))] * 2,
        compiler_params=pltpu.CompilerParams(collective_id=1, has_side_effects=True),
    )(offsets, slots, backward, twists, probe)


def project_kernel(sketch_ref, inverse_ref, moment_ref, out_ref):
    factors = jnp.dot(
        sketch_ref[0].astype(F32), inverse_ref[0],
        precision=lax.Precision.HIGHEST, preferred_element_type=F32,
    ).astype(BF16)
    _, parts, _, width = moment_ref.shape
    for p in range(parts):
        out_ref[0, :, p * width : (p + 1) * width] = jnp.dot(
            factors, moment_ref[:, p].reshape(RANK, width), preferred_element_type=F32
        ).astype(BF16)


def projected(sketches, inverses, moments):
    many, count, _ = sketches.shape
    parts, width = moments.shape[1], moments.shape[3]

    def per(*shape):
        return pl.BlockSpec((1,) + shape, lambda o: (o,) + (0,) * len(shape))

    return pl.pallas_call(
        project_kernel,
        name="projected",
        grid=(many,),
        out_shape=jax.ShapeDtypeStruct((many, count, parts * width), BF16),
        in_specs=[
            per(count, RANK), per(RANK, RANK),
            pl.BlockSpec((SPLIT, parts, RANK // SPLIT, width), lambda o: (o, 0, 0, 0)),
        ],
        out_specs=per(count, parts * width),
    )(sketches, inverses, moments)


def body(traces, alive, offsets, probe):
    peers = lax.axis_size("fibre")
    count, total = traces.shape
    assert WINDOW == 4 * count and peers % 4 == 0
    forward, backward, twists = tables(total)
    slots = spectra(traces, alive, forward, twists, peers)
    correlations, sketches, moments, inverses = reduced(
        offsets, slots, backward, twists, probe.T, peers
    )
    return (correlations, projected(sketches, inverses, moments))


def solution(mesh):
    placed = (P(("groups", "fibre"), None), P(("groups", "fibre")), P(), P())
    return jax.shard_map(
        body,
        mesh=mesh,
        in_specs=placed,
        out_specs=(P(None, ("groups", "fibre"), None), P(None, ("groups", "fibre"), None)),
        check_vma=False,
    )
```

```python
import functools
import math

import jax
import jax.numpy as jnp
import numpy as np
from jax import lax
from jax.experimental import pallas as pl
from jax.experimental.pallas import tpu as pltpu
from jax.sharding import PartitionSpec as P

RANK = 64
WINDOW = 256
LANES = 128
ROWS = 16
SPLIT = 2
PIECES = 2
OTHERS = (0, 3)
F32 = jnp.float32
BF16 = jnp.bfloat16
MESH = pl.DeviceIdType.MESH


def tables(total):
    radix = total // LANES
    half = radix // 2 + 1
    n = np.arange(LANES)
    angle = 2.0 * math.pi * ((n[:, None] * n[None, :]) % LANES) / LANES
    cosine, sine = np.cos(angle), np.sin(angle)
    forward = np.block([[cosine, -sine], [sine, cosine]])
    backward = np.block([[cosine, sine], [-sine, cosine]])
    twist = 2.0 * math.pi * np.arange(half)[:, None] * n[None, :] / total
    twists = np.stack([np.cos(twist), np.sin(twist)])[:, :, None, :]
    return (
        jnp.asarray(forward, BF16),
        jnp.asarray(backward, BF16),
        jnp.asarray(twists, F32),
    )


def add(a, b):
    return b if a is None else (a if b is None else a + b)


def sub(a, b):
    if b is None:
        return a
    return -b if a is None else a - b


def turn(value, k, n, sign):
    re, im = value
    if k == 0:
        return value
    c, s = math.cos(2 * math.pi * k / n), sign * math.sin(2 * math.pi * k / n)
    if abs(c) < 1e-12:
        if s > 0:
            return (None if im is None else -im, re)
        return (im, None if re is None else -re)
    if im is None:
        return (re * c, re * s)
    if abs(abs(c) - abs(s)) < 1e-12:
        r = abs(c)
        a, b = math.copysign(1, c), math.copysign(1, s)
        x = (re if a > 0 else -re) - (im if b > 0 else -im)
        y = (re if b > 0 else -re) + (im if a > 0 else -im)
        return (x * r, y * r)
    return (re * c - im * s, re * s + im * c)


def real_forward(x):
    n = len(x)
    if n == 1:
        return [(x[0], None)]
    if n == 2:
        return [(x[0] + x[1], None), (x[0] - x[1], None)]
    even, odd = real_forward(x[0::2]), real_forward(x[1::2])
    out = [None] * (n // 2 + 1)
    for k in range(n // 4 + 1):
        e, o = even[k], turn(odd[k], k, n, -1.0)
        out[k] = (add(e[0], o[0]), add(e[1], o[1]))
        if n // 2 - k != k:
            low = (sub(e[0], o[0]), sub(e[1], o[1]))
            out[n // 2 - k] = (low[0], None if low[1] is None else -low[1])
    return out


def real_backward(v):
    n = 2 * (len(v) - 1)
    if n == 2:
        return [v[0][0] + v[1][0], v[0][0] - v[1][0]]
    even, odd = [], []
    for k in range(n // 4 + 1):
        a, b = v[k], v[n // 2 - k]
        if k == 0:
            even.append((a[0] + b[0], None))
            odd.append((a[0] - b[0], None))
        elif k == n // 4:
            even.append((a[0] + a[0], None))
            odd.append((-(a[1] + a[1]), None))
        else:
            even.append((a[0] + b[0], a[1] - b[1]))
            odd.append(turn((a[0] - b[0], a[1] + b[1]), k, n, 1.0))
    out = [None] * n
    out[0::2] = real_backward(even)
    out[1::2] = real_backward(odd)
    return out


def spectra_kernel(
    peers, x_ref, alive_ref, forward_ref, twist_ref, slots, turned, wide,
    core_s, core_r, z_s, z_r, y_s, y_r, relay_s, relay_r, done_s, done_r,
):
    count, total = x_ref.shape
    radix = total // LANES
    half = radix // 2 + 1
    groups = count // ROWS
    me = lax.axis_index("fibre")
    core = lax.rem(me, 2)
    chip = me // 2
    odd = lax.rem(chip, 2)
    pair = me + 1 - 2 * core
    across = me + 2 - 4 * odd
    upper, lower = me + 4, me - 4
    has_upper, has_lower = me < peers - 4, me >= 4
    barrier = pltpu.get_barrier_semaphore()
    for peer in (pair, across):
        pl.semaphore_signal(barrier, inc=1, device_id={"fibre": peer}, device_id_type=MESH)

    @pl.when(has_upper)
    def _():
        pl.semaphore_signal(barrier, inc=1, device_id={"fibre": upper}, device_id_type=MESH)

    @pl.when(has_lower)
    def _():
        pl.semaphore_signal(barrier, inc=1, device_id={"fibre": lower}, device_id_type=MESH)

    shape = (count, count)
    eye = lax.broadcasted_iota(jnp.int32, shape, 0) == lax.broadcasted_iota(jnp.int32, shape, 1)
    alive = jnp.where(eye, jnp.broadcast_to(alive_ref[...].astype(F32), shape), 0.0)
    alive = jnp.broadcast_to(jnp.sum(alive, axis=1, keepdims=True), (count, LANES))

    def move(source, target, send, recv, index, peer):
        return pltpu.make_async_remote_copy(
            src_ref=slots.at[source, index // PIECES, pl.ds(*spans[index % PIECES])],
            dst_ref=slots.at[target, index // PIECES, pl.ds(*spans[index % PIECES])],
            send_sem=send.at[index],
            recv_sem=recv.at[index],
            device_id={"fibre": peer},
            device_id_type=MESH,
        )

    own, nearer, farther = core, 2 + core, 4 + core
    cuts = [half * i // PIECES for i in range(PIECES + 1)]
    spans = [(a, b - a) for a, b in zip(cuts[:-1], cuts[1:])]
    for index in range(groups):
        rows = slice(index * ROWS, (index + 1) * ROWS)
        x = [x_ref[rows, a * LANES : (a + 1) * LANES].astype(F32) for a in range(radix)]
        squares = x[0] * x[0]
        for a in range(1, radix):
            squares = squares + x[a] * x[a]
        energy = jnp.sum(squares, axis=1, keepdims=True)
        level = jnp.broadcast_to(0.1 * (energy + 1e-05), (ROWS, LANES))
        for k, (re, im) in enumerate(real_forward(x)):
            cosine, sine = twist_ref[0, k], twist_ref[1, k]
            if im is None:
                turned[k, :, :LANES] = (re * cosine).astype(BF16)
                turned[k, :, LANES:] = (-(re * sine)).astype(BF16)
            else:
                turned[k, :, :LANES] = (re * cosine + im * sine).astype(BF16)
                turned[k, :, LANES:] = (im * cosine - re * sine).astype(BF16)
        stacked = turned[...].reshape(half * ROWS, 2 * LANES)
        wide[...] = jnp.dot(stacked, forward_ref[...], preferred_element_type=F32)
        for k in range(half):
            at = slice(k * ROWS, (k + 1) * ROWS)
            re, im = wide[at, :LANES], wide[at, LANES:]
            scale = alive[rows] * lax.rsqrt(re * re + im * im + level)
            slots[own, index, k, :, :LANES] = (re * scale).astype(BF16)
            slots[own, index, k, :, LANES:] = (im * scale).astype(BF16)
        if index == 0:
            met = 2 + has_upper.astype(jnp.int32) + has_lower.astype(jnp.int32)
            pl.semaphore_wait(barrier, met)

        for piece in range(index * PIECES, (index + 1) * PIECES):
            @pl.when(has_lower)
            def _():
                move(own, farther, z_s, z_r, piece, lower).start()

            @pl.when(odd == 1)
            def _():
                move(own, nearer, y_s, y_r, piece, across).start()

            move(own, own, core_s, core_r, piece, pair).start()

    @pl.when(jnp.logical_not(has_upper))
    def _():
        for index in range(groups):
            for k in range(half):
                slots[farther, index, k] = jnp.zeros((ROWS, 2 * LANES), BF16)

    for index in range(groups * PIECES):
        @pl.when(has_upper)
        def _():
            move(own, farther, z_s, z_r, index, lower).wait_recv()

        @pl.when(odd == 0)
        def _():
            move(farther, nearer, y_s, y_r, index, across).start()

        move(farther, farther, done_s, done_r, index, pair).start()
        move(own, nearer, y_s, y_r, index, across).wait_recv()
        move(nearer, nearer, relay_s, relay_r, index, pair).start()
    for index in range(groups * PIECES):
        move(own, own, core_s, core_r, index, pair).wait()
        move(farther, farther, done_s, done_r, index, pair).wait()
        move(nearer, nearer, relay_s, relay_r, index, pair).wait()
        move(own, nearer, y_s, y_r, index, across).wait_send()

        @pl.when(has_lower)
        def _():
            move(own, farther, z_s, z_r, index, lower).wait_send()


def spectra(traces, alive, forward, twists, peers):
    count, total = traces.shape
    half = total // LANES // 2 + 1
    groups = count // ROWS
    vmem = pl.BlockSpec(memory_space=pltpu.VMEM)
    return pl.pallas_call(
        functools.partial(spectra_kernel, peers),
        name="spectra",
        out_shape=jax.ShapeDtypeStruct((6, groups, half, ROWS, 2 * LANES), BF16),
        in_specs=[vmem] * 4,
        out_specs=vmem,
        scratch_shapes=[
            pltpu.VMEM((half, ROWS, 2 * LANES), BF16),
            pltpu.VMEM((half * ROWS, 2 * LANES), F32),
        ]
        + [pltpu.SemaphoreType.DMA((groups * PIECES,))] * 10,
        compiler_params=pltpu.CompilerParams(collective_id=0, has_side_effects=True),
    )(traces, alive.reshape(1, count), forward, twists)


def make_panel(
    o, offsets_ref, slots, backward_ref, twist_ref, probe_ref, panel_ref, sketch_ref,
    moment_ref, cross, inner, wide,
):
    half, count = slots.shape[2], slots.shape[1] * slots.shape[3]
    radix = 2 * (half - 1)
    total = radix * LANES
    core = lax.rem(lax.axis_index("fibre"), 2)
    start = core * count + offsets_ref[o]
    block = start // count
    shift = start - block * count
    after = jnp.minimum(block + 1, 5)
    shape = (count, count)
    gap = lax.broadcasted_iota(jnp.int32, shape, 1) - lax.broadcasted_iota(jnp.int32, shape, 0)
    first = jnp.where(gap == shift, 1.0, 0.0).astype(BF16)
    second = jnp.where(gap == shift - count, 1.0, 0.0).astype(BF16)
    pick = jnp.concatenate([first, second], axis=1)
    for k in range(half):
        flat = (count, 2 * LANES)
        both = [slots[block, :, k].reshape(flat), slots[after, :, k].reshape(flat)]
        both = jnp.concatenate(both, axis=0)
        other = jnp.dot(pick, both, preferred_element_type=F32)
        own = slots[core, :, k].reshape(flat).astype(F32)
        a, b = own[:, :LANES], own[:, LANES:]
        c, d = other[:, :LANES], other[:, LANES:]
        cross[k, :, :LANES] = (a * c + b * d).astype(BF16)
        cross[k, :, LANES:] = (b * c - a * d).astype(BF16)
    stacked = cross[...].reshape(half * count, 2 * LANES)
    inner[...] = jnp.dot(stacked, backward_ref[...], preferred_element_type=F32)
    for k in range(half):
        at = slice(k * count, (k + 1) * count)
        re, im = inner[at, :LANES], inner[at, LANES:]
        cosine, sine = twist_ref[0, k], twist_ref[1, k]
        wide[k, :, :LANES] = re * cosine - im * sine
        if 0 < k < half - 1:
            wide[k, :, LANES:] = re * sine + im * cosine

    @pl.loop(0, count // ROWS)
    def _(step):
        rows = pl.ds(pl.multiple_of(step * ROWS, ROWS), ROWS)
        values = []
        for k in range(half):
            inside = 0 < k < half - 1
            values.append((wide[k, rows, :LANES], wide[k, rows, LANES:] if inside else None))
        for a, out in enumerate(real_backward(values)):
            panel_ref[o, rows, a * LANES : (a + 1) * LANES] = (out * total**-0.5).astype(BF16)

    sketch = lax.dot_general(
        panel_ref[o], probe_ref[...], (((1,), (1,)), ((), ())), preferred_element_type=F32
    )
    flipped = sketch.T.astype(BF16)
    sketch = sketch.astype(BF16)
    sketch_ref[o] = sketch
    gram = jnp.dot(flipped, sketch, preferred_element_type=F32)
    parts, tall, width = moment_ref.shape[1:]
    split = RANK // tall
    for p in range(parts):
        columns = panel_ref[o, :, p * width : (p + 1) * width]
        moments = jnp.dot(flipped, columns, preferred_element_type=F32).astype(BF16)
        for h in range(split):
            moment_ref[o * split + h, p] = moments[h * tall : (h + 1) * tall]
    return gram


def eliminate(matrix, pivots):
    shape = matrix.shape
    row_at = lax.broadcasted_iota(jnp.int32, shape, 1)
    column_at = lax.broadcasted_iota(jnp.int32, shape, 2)
    for k in pivots:
        row = matrix[:, k : k + 1, :]
        on_column = column_at == k
        column = jnp.sum(jnp.where(on_column, matrix, 0.0), axis=2, keepdims=True)
        pivot = 1.0 / column[:, k : k + 1, :]
        scaled = jnp.where(on_column[:, :1, :], pivot, row * pivot)
        matrix = jnp.where(
            row_at == k, scaled, jnp.where(on_column, 0.0, matrix) - column * scaled
        )
    return matrix


def orders(peers, many):
    bits = [1 << i for i in range(peers.bit_length() - 1)]
    other = bits[:1] + bits[2:] + bits[1:2]
    return [other if o in OTHERS else bits for o in range(many)]


def reduce_kernel(
    peers, offsets_ref, slots, backward_ref, twist_ref, probe_ref, panel_ref, sketch_ref, full,
    inverse_ref, cross, inner, wide, moment_ref, sums, landed, grams, gram_in,
    rs_s, rs_r, ag_s, ag_r, g_s, g_r,
):
    many = moment_ref.shape[0]
    plan = orders(peers, many)
    steps = len(plan[0])
    me = lax.axis_index("fibre")

    def bit_of(bit):
        return lax.rem(me // bit, 2)

    def partner(bit):
        return me + bit - 2 * bit * bit_of(bit)

    several = panel_ref.shape[0]
    barrier = pltpu.get_barrier_semaphore()
    for bit in plan[0]:
        pl.semaphore_signal(barrier, inc=1, device_id={"fibre": partner(bit)}, device_id_type=MESH)

    def remote(src, dst, send, recv, peer):
        return pltpu.make_async_remote_copy(
            src_ref=src, dst_ref=dst, send_sem=send, recv_sem=recv,
            device_id={"fibre": peer}, device_id_type=MESH,
        )

    low = [[0] for _ in range(many)]
    for o in range(many):
        for s in range(steps):
            low[o].append(low[o][s] + bit_of(plan[o][s]) * (peers >> (s + 1)))
    base = [peers - (peers >> s) for s in range(steps)]

    def halve(o, s):
        size = peers >> (s + 1)
        bit = plan[o][s]
        theirs = low[o][s] + (1 - bit_of(bit)) * size
        source = moment_ref if s == 0 else sums
        return remote(
            source.at[o, pl.ds(theirs, size)], landed.at[o, pl.ds(base[s], size)],
            rs_s.at[o, s], rs_r.at[o, s], partner(bit),
        )

    def double(s):
        return remote(grams.at[s], gram_in.at[s], g_s.at[s], g_r.at[s], partner(plan[0][s]))

    def gather(o, s):
        size = peers >> (s + 1)
        here = full.at[o, pl.ds(low[o][s + 1], size)]
        return remote(here, here, ag_s.at[o, s], ag_r.at[o, s], partner(plan[o][s]))

    def advance(o, s):
        size = peers >> (s + 1)
        last = s == steps - 1
        halve(o, s).wait_recv()
        source = moment_ref if s == 0 else sums
        target = full if last else sums
        for p in range(size):
            at = low[o][s + 1] + p
            value = source[o, at].astype(F32) + landed[o, base[s] + p].astype(F32)
            target[o, at] = value.astype(BF16)
        if last:
            gather(o, s).start()
        else:
            halve(o, s + 1).start()

    split = many // several
    reached = [0] * many
    loose = []
    for panel in range(several):
        loose.append(
            make_panel(
                panel, offsets_ref, slots, backward_ref, twist_ref, probe_ref, panel_ref,
                sketch_ref, moment_ref, cross, inner, wide,
            )
        )
        if panel == 0:
            pl.semaphore_wait(barrier, steps)
        for o in range(panel * split, (panel + 1) * split):
            halve(o, 0).start()
        if panel == several - 1:
            loose = jnp.concatenate(loose, axis=0)
            tall = several * RANK
            grams[0] = jnp.concatenate([loose[: tall // 2], loose[tall // 2 :]], axis=1)
            double(0).start()
        for o in range(panel * split):
            if reached[o] < steps - 1:
                advance(o, reached[o])
                reached[o] += 1
    for s in range(steps):
        last = s == steps - 1
        for o in range(many):
            if reached[o] == s:
                advance(o, s)
                reached[o] += 1
        double(s).wait_recv()
        total = grams[s] + gram_in[s]
        if last:
            loose = jnp.concatenate([total[:, :RANK], total[:, RANK:]], axis=0)
            matrix = loose.reshape(several, RANK, RANK)
        else:
            grams[s + 1] = total
            double(s + 1).start()
    share = -(-RANK // steps)
    for s in reversed(range(steps)):
        at = (steps - 1 - s) * share
        matrix = eliminate(matrix, range(at, min(at + share, RANK)))
        for o in range(many):
            gather(o, s).wait_recv()
            if s > 0:
                gather(o, s - 1).start()
    inverse_ref[...] = matrix
    for s in range(steps):
        double(s).wait_send()
        for o in range(many):
            halve(o, s).wait_send()
            gather(o, s).wait_send()


def reduced(offsets, slots, backward, twists, probe, peers):
    _, groups, half, rows, _ = slots.shape
    count = groups * rows
    total = probe.shape[1]
    several = offsets.shape[0]
    many = several * SPLIT
    steps = peers.bit_length() - 1
    moments = (many, peers, RANK // SPLIT, total // peers)
    packed = (steps, several * RANK // 2, 2 * RANK)
    vmem = pl.BlockSpec(memory_space=pltpu.VMEM)
    dma = pltpu.SemaphoreType.DMA
    return pl.pallas_call(
        functools.partial(reduce_kernel, peers),
        name="reduced",
        out_shape=(
            jax.ShapeDtypeStruct((several, count, total), BF16),
            jax.ShapeDtypeStruct((several, count, RANK), BF16),
            jax.ShapeDtypeStruct(moments, BF16),
            jax.ShapeDtypeStruct((several, RANK, RANK), F32),
        ),
        in_specs=[pl.BlockSpec(memory_space=pltpu.SMEM)] + [vmem] * 4,
        out_specs=(vmem,) * 4,
        scratch_shapes=[
            pltpu.VMEM((half, count, 2 * LANES), BF16),
            pltpu.VMEM((half * count, 2 * LANES), F32),
            pltpu.VMEM((half, count, 2 * LANES), F32),
            pltpu.VMEM(moments, BF16),
            pltpu.VMEM(moments, BF16),
            pltpu.VMEM(moments, BF16),
            pltpu.VMEM(packed, F32),
            pltpu.VMEM(packed, F32),
        ]
        + [dma((many, steps))] * 4
        + [dma((steps,))] * 2,
        compiler_params=pltpu.CompilerParams(collective_id=1, has_side_effects=True),
    )(offsets, slots, backward, twists, probe)


def project_kernel(sketch_ref, inverse_ref, moment_ref, out_ref):
    factors = jnp.dot(
        sketch_ref[0].astype(F32), inverse_ref[0],
        precision=lax.Precision.HIGHEST, preferred_element_type=F32,
    ).astype(BF16)
    _, parts, _, width = moment_ref.shape
    for p in range(parts):
        out_ref[0, :, p * width : (p + 1) * width] = jnp.dot(
            factors, moment_ref[:, p].reshape(RANK, width), preferred_element_type=F32
        ).astype(BF16)


def projected(sketches, inverses, moments):
    many, count, _ = sketches.shape
    parts, width = moments.shape[1], moments.shape[3]

    def per(*shape):
        return pl.BlockSpec((1,) + shape, lambda o: (o,) + (0,) * len(shape))

    return pl.pallas_call(
        project_kernel,
        name="projected",
        grid=(many,),
        out_shape=jax.ShapeDtypeStruct((many, count, parts * width), BF16),
        in_specs=[
            per(count, RANK), per(RANK, RANK),
            pl.BlockSpec((SPLIT, parts, RANK // SPLIT, width), lambda o: (o, 0, 0, 0)),
        ],
        out_specs=per(count, parts * width),
    )(sketches, inverses, moments)


def body(traces, alive, offsets, probe):
    peers = lax.axis_size("fibre")
    count, total = traces.shape
    assert WINDOW == 4 * count and peers % 4 == 0
    forward, backward, twists = tables(total)
    slots = spectra(traces, alive, forward, twists, peers)
    correlations, sketches, moments, inverses = reduced(
        offsets, slots, backward, twists, probe.T, peers
    )
    return (correlations, projected(sketches, inverses, moments))


def solution(mesh):
    placed = (P(("groups", "fibre"), None), P(("groups", "fibre")), P(), P())
    return jax.shard_map(
        body,
        mesh=mesh,
        in_specs=placed,
        out_specs=(P(None, ("groups", "fibre"), None), P(None, ("groups", "fibre"), None)),
        check_vma=False,
    )
```
